32 devices in a mesh: cell: 8 (over z, y), region: 4 (over x, core).
Axes of the slice: x: 2, y: 2, z: 4, core: 2. Of those that a mesh axis runs over, the one named last changes fastest.
Arguments:
- observed: bfloat16 [8192, 16384], P('cell', 'region'), may hold values from -0.5 to 0.5
- block_mask: int32 [1024, 128], P('cell', 'region'), may hold values 0 or 1
- plan: int32 [4], replicated, may hold values from 0 to 3, each once
- cell_factors: float32 [8192, 256], P('cell'), may hold values from -6 to 6
- region_factors: float32 [32768, 256], P(('cell', 'region')), may hold values from -6 to 6
Outputs:
- new_cells: float32 [8192, 256], P('cell')
- new_regions: float32 [32768, 256], P(('cell', 'region'))
The draws below stay inside these ranges and needn't reach their ends.
Inputs may be any that keep to these rules, and one draw needn't show every extreme that they name: `plan`: each stored slot 0 to 3 appears once.
All inputs are finite; a program needn't handle non-finite values. No bound on the sum of `block_mask` on one device may be relied on, other than what follows from the above.
Results may differ from the reference program's by a relative error of at most 0.0056.
Values sent between devices are 32-bit elements; how exact they have to be, the bound alone decides.
No kernel may reach another device: no remote copies, remote signals or barrier semaphores. Data moves between devices by JAX's collectives and lax.ppermute only.
A program may use at most 64 MiB of HBM per device.

```python
import math
import jax
import jax.numpy as jnp
from jax import lax

K = 256
CELL_DEV = 1024
SUB = 1024
STRATA = 4
CELLS = 8192
REGION_BLOCKS = 32
WINDOW_COLS = 16384
N_CELL = 8
N_REGION = 4


def plant(array, stream_key, least, top_value):
    longest = array.shape.index(max(array.shape))
    spots = []
    for shift in (0, 1):
        where = [jax.random.randint(jax.random.fold_in(stream_key, axis), (), 0, length) for axis, length in enumerate(array.shape)]
        where[longest] = (where[longest] + shift) % array.shape[longest]
        spots.append(tuple(where))
    return array.at[spots[0]].set(least).at[spots[1]].set(top_value)


def levels(stream_key, shape, cuts, low, high):
    def one(axis_at, parts):
        heights = jax.random.uniform(jax.random.fold_in(jax.random.fold_in(stream_key, 6), axis_at), (parts,), jnp.float32, low / len(cuts), high / len(cuts))
        return jnp.repeat(jnp.exp(heights), shape[axis_at] // parts).reshape((-1,) + (1,) * (len(shape) - axis_at - 1))

    level = one(*cuts[0])
    for cut in cuts[1:]:
        level = level * one(*cut)
    return level


def scatter_about(stream_key, dims, width, reach, cuts=(), held_as=jnp.bfloat16):
    array = jax.random.normal(stream_key, dims, jnp.float32) * width
    if len(cuts) > 0:
        array = levels(stream_key, dims, cuts, -0.22, 0.18) * array
    return jnp.clip(array, min=-reach, max=reach).astype(held_as)


def setup_inputs(seed: int = 0) -> dict:
    key_of = jax.random.split(jax.random.key(seed), 6)
    return {
        "observed": jnp.clip(jax.random.uniform(key_of[0], (CELLS, WINDOW_COLS), jnp.float32, -0.5, 0.5) * levels(key_of[0], (CELLS, WINDOW_COLS), ((0, 8), (1, 4)), -0.4, 0.0), -0.5, 0.5).astype(jnp.bfloat16),
        "block_mask": plant((jax.random.randint(key_of[1], (CELLS // 8, WINDOW_COLS // 128), 0, 5) < 3).astype(jnp.int32), jax.random.fold_in(key_of[1], 1), 0, 1),
        "plan": jax.random.permutation(key_of[2], STRATA).astype(jnp.int32),
        "cell_factors": scatter_about(key_of[3], (CELLS, K), 1.0, 6.0, ((0, 8),), jnp.float32),
        "region_factors": scatter_about(key_of[4], (REGION_BLOCKS * SUB, K), 1.0, 6.0, ((0, 32),), jnp.float32),
    }


beta_mom = 0.9

def reference(observed, block_mask, plan, cell_factors, region_factors):
    total_cols = N_REGION * SUB
    scale_pred = 0.5 / math.sqrt(total_cols)
    rate_region = total_cols / CELL_DEV
    data_tiles = observed.reshape(N_CELL, CELL_DEV, N_REGION, STRATA, SUB)
    mask_tiles = block_mask.reshape(N_CELL, CELL_DEV // 8, N_REGION, STRATA, SUB // 128)
    cells_now = cell_factors.reshape(N_CELL, CELL_DEV, K)
    regions_now = region_factors.reshape(N_CELL, N_REGION, SUB, K)
    momentum = jnp.zeros_like(cells_now)

    def block_grads(items):
        cell_rows, data_block, mask_block, region_block = items
        cell_bf = cell_rows.astype(jnp.bfloat16).astype(jnp.float32)
        region_bf = region_block.astype(jnp.bfloat16).astype(jnp.float32)
        predicted = jnp.einsum('rk,jck->rjc', cell_bf, region_bf)
        expanded = jnp.broadcast_to(mask_block[:, None, :, :, None], (CELL_DEV // 8, 8, N_REGION, SUB // 128, 128))
        expanded = expanded.reshape(CELL_DEV, N_REGION, SUB).astype(jnp.float32)
        resid = (expanded * (scale_pred * predicted - data_block.astype(jnp.float32))).astype(jnp.bfloat16)
        resid_f = resid.astype(jnp.float32)
        grad_cell = scale_pred * jnp.einsum('rjc,jck->rk', resid_f, region_bf)
        grad_region = scale_pred * jnp.einsum('rjc,rk->jck', resid_f, cell_bf)
        return (grad_cell, grad_region)
    for section in range(STRATA):
        slot_index = plan[section]
        data_slot = lax.dynamic_index_in_dim(data_tiles, slot_index, 3, keepdims=False)
        mask_slot = lax.dynamic_index_in_dim(mask_tiles, slot_index, 3, keepdims=False)
        chosen = jnp.roll(regions_now, -section, axis=0)
        grad_cells, grad_regions = lax.map(block_grads, (cells_now, data_slot, mask_slot, chosen))
        regions_now = regions_now - rate_region * jnp.roll(grad_regions, section, axis=0)
        momentum = beta_mom * momentum + grad_cells
        cells_now = cells_now - momentum
    return (cells_now.reshape(CELLS, K), regions_now.reshape(REGION_BLOCKS * SUB, K))
```

```python
import functools
import math

import jax
import jax.numpy as jnp
from jax import lax
from jax.experimental import pallas as pl
from jax.experimental.pallas import tpu as pltpu
from jax.sharding import PartitionSpec as P


STRATA = 4
CHUNKS = 2
LANES = 128
MASK_ROWS = 8


beta_mom = 0.9


def permuted(value, axis, to):
    count = lax.axis_size(axis)
    pairs = [(source, to(source) % count) for source in range(count)]
    return lax.ppermute(value, axis, pairs)


def nt_dot(a, b):
    return lax.dot_general(a, b, (((1,), (1,)), ((), ())), preferred_element_type=jnp.float32)


def tn_dot(a, b):
    return lax.dot_general(a, b, (((0,), (0,)), ((), ())), preferred_element_type=jnp.float32)


def block_kernel(cfg, plan, observed, mask, *refs):
    section, chunk, scale, rate = cfg
    opening, first, last = section == 0, chunk == 0, chunk == CHUNKS - 1
    refs = list(refs)

    def take(count):
        got = refs[:count]
        del refs[:count]
        return got

    if first and opening:
        (cells_hbm,) = take(1)
    elif first:
        cells_ref, mom_mine, mom_other = take(3)
    else:
        cells_bf, grad_in = take(2)
    (region_ref,) = take(1)
    (new_region,) = take(1)
    if first and not opening:
        (new_cells,) = take(1)
    if first:
        (cells_bf,) = take(1)
    grads = take(2 if last else 1)
    data, wide, resid, sems = take(4)
    side = lax.axis_index("region") % 2
    slot = plan[section]
    cell_rows, m = data.shape
    half = cell_rows // 2
    tile = min(256, half)
    tiles = cell_rows // tile
    columns = mask.shape[1] // STRATA

    def fetch(source, target, at):
        copy = pltpu.make_async_copy(source, target, sems.at[at])
        copy.start()
        return copy

    if opening:
        region_buf = refs.pop(0)
        region_copy = fetch(region_ref.at[pl.ds(chunk * m, m), :], region_buf, tiles)
        if first:
            cells_buf = refs.pop(0)
            cells_copy = fetch(cells_hbm, cells_buf, tiles + 1)
        region_ref = region_buf
    start = pl.multiple_of(slot * (m * CHUNKS) + chunk * m, LANES)
    copies = [
        fetch(
            observed.at[pl.ds(i * tile, tile), pl.ds(start, m)],
            data.at[pl.ds(i * tile, tile), :],
            i,
        )
        for i in range(tiles)
    ]
    wanted = slot * columns + chunk * (m // LANES) + lax.broadcasted_iota(
        jnp.int32, (mask.shape[1], m), 1
    ) // LANES
    pick = wanted == lax.broadcasted_iota(jnp.int32, (mask.shape[1], m), 0)
    wide[...] = jnp.dot(
        mask[...].astype(jnp.bfloat16),
        pick.astype(jnp.float32).astype(jnp.bfloat16),
        preferred_element_type=jnp.float32,
    )
    if first and opening:
        cells_copy.wait()
        cells_bf[...] = cells_buf[...].astype(jnp.bfloat16)
    elif first:
        for who, mom in ((1 - side, mom_other), (side, mom_mine)):
            rows = pl.ds(pl.multiple_of(who * half, half), half)
            now = cells_ref[rows, :] - mom[...]
            new_cells[rows, :] = now
            cells_bf[rows, :] = now.astype(jnp.bfloat16)
    if opening:
        region_copy.wait()
    region_bf = region_ref[...].astype(jnp.bfloat16)
    for i in range(tiles):
        predicted = nt_dot(cells_bf[i * tile : (i + 1) * tile, :], region_bf)
        copies[i].wait()
        step = 2 * MASK_ROWS
        for r in range(0, tile, step):
            at = i * tile + r
            w = [
                jnp.broadcast_to(wide[(at + d) // MASK_ROWS : (at + d) // MASK_ROWS + 1, :], (MASK_ROWS, m))
                for d in range(0, step, MASK_ROWS)
            ]
            w = jnp.concatenate(w, 0)
            value = scale * predicted[r : r + step, :] - data[at : at + step, :].astype(jnp.float32)
            resid[at : at + step, :] = (w * value).astype(jnp.bfloat16)
    for i in range(tiles):
        per_half = tiles // 2
        if last:
            who = (1 - side) if i < per_half else side
            rows = pl.ds(pl.multiple_of(who * half + (i % per_half) * tile, tile), tile)
            target = grads[i // per_half].at[pl.ds((i % per_half) * tile, tile), :]
        else:
            rows = pl.ds(i * tile, tile)
            target = grads[0].at[rows, :]
        grad = scale * jnp.dot(resid[rows, :], region_bf, preferred_element_type=jnp.float32)
        if not first:
            grad = grad + grad_in[rows, :]
        target[...] = grad
    hsum = tn_dot(resid[...], cells_bf[...])
    new_region[...] = region_ref[...] - rate * (scale * hsum)


def block_call(section, chunk, scale, rate, plan, observed, mask, ins, region):
    opening, first, last = section == 0, chunk == 0, chunk == CHUNKS - 1
    rank = region.shape[1]
    m = region.shape[0] // CHUNKS if opening else region.shape[0]
    cell_rows = observed.shape[0]
    f32, bf16 = jnp.float32, jnp.bfloat16
    vm = pl.BlockSpec(memory_space=pltpu.VMEM)
    hbm = pl.BlockSpec(memory_space=pltpu.HBM)
    whole = (cell_rows, rank)
    outs = [jax.ShapeDtypeStruct((m, rank), f32)]
    if first and not opening:
        outs += [jax.ShapeDtypeStruct(whole, f32)]
    if first:
        outs += [jax.ShapeDtypeStruct(whole, bf16)]
    if last:
        outs += [jax.ShapeDtypeStruct((cell_rows // 2, rank), f32)] * 2
    else:
        outs += [jax.ShapeDtypeStruct(whole, f32)]
    scratch = [
        pltpu.VMEM((cell_rows, m), observed.dtype),
        pltpu.VMEM((mask.shape[0], m), f32),
        pltpu.VMEM((cell_rows, m), bf16),
        pltpu.SemaphoreType.DMA((16,)),
    ]
    if opening:
        scratch.append(pltpu.VMEM((m, rank), f32))
        if first:
            scratch.append(pltpu.VMEM(whole, f32))
    args = (plan, observed, mask, *ins, region)
    return pl.pallas_call(
        functools.partial(block_kernel, (section, chunk, scale, rate)),
        out_shape=outs,
        in_specs=[pl.BlockSpec(memory_space=pltpu.SMEM), hbm, vm]
        + [hbm if opening and first else vm] * len(ins)
        + [hbm if opening else vm],
        out_specs=[vm] * len(outs),
        scratch_shapes=scratch,
        compiler_params=pltpu.CompilerParams(vmem_limit_bytes=54 << 20),
        cost_estimate=pl.CostEstimate(
            flops=6 * cell_rows * m * rank, bytes_accessed=4 << 20, transcendentals=0
        ),
    )(*args)


def summed(value, bits, index, tag):
    bit = bits[0]
    if len(bits) == 1:
        return value + permuted(value, "region", lambda i: i ^ bit)
    side = (index // bit) % 2
    rows = value.shape[0] // 2
    mine = lax.dynamic_slice_in_dim(value, side * rows, rows, 0)
    send = lax.dynamic_slice_in_dim(value, (1 - side) * rows, rows, 0)
    mine = mine + permuted(send, "region", lambda i: i ^ bit)
    mine = summed(mine, bits[1:], index, tag)
    other = permuted(mine, "region", lambda i: i ^ bit)
    return jnp.concatenate(
        [jnp.where(side == 0, mine, other), jnp.where(side == 0, other, mine)], 0
    )


def returned(chunks):
    steps = STRATA - 1
    count = lax.axis_size("cell")
    odd = lax.axis_index("cell") % 2 == 1
    rows = chunks[0].shape[0]
    part = rows * len(chunks) // 4
    relay = permuted(chunks[0][:part], "cell", lambda i: i - 1 if i % 2 else i + steps)
    outs = []
    for k, chunk in enumerate(chunks):
        piece = chunk[part:] if k == 0 else chunk
        if piece.shape[0]:
            outs.append(permuted(piece, "cell", lambda i: i + steps))
    final = lax.ppermute(relay, "cell", [(i, (i + steps + 1) % count) for i in range(0, count, 2)])
    return jnp.concatenate([jnp.where(odd, relay, final)] + outs, 0)


def body(observed, block_mask, plan, cell_factors, region_factors):
    n_region = lax.axis_size("region")
    index = lax.axis_index("region")
    bits = [1 << p for p in range(n_region.bit_length() - 1)]
    side = index % 2
    cell_rows, _ = cell_factors.shape
    block_rows = region_factors.shape[0]
    total_cols = n_region * block_rows
    scale = 0.5 / math.sqrt(total_cols)
    rate = total_cols / cell_rows
    cells_now = cell_factors
    chunks = [region_factors] * CHUNKS
    mom_mine = mom_other = None
    for s in range(STRATA):
        grad = None
        sent = []
        for k in range(CHUNKS):
            if k == 0:
                ins = (cells_now,) if s == 0 else (cells_now, mom_mine, mom_other)
            else:
                ins = (cells_bf, grad)
            outs = block_call(s, k, scale, rate, plan, observed, block_mask, ins, chunks[k])
            new_chunk, outs = outs[0], outs[1:]
            if k == 0 and s > 0:
                cells_now, outs = outs[0], outs[1:]
            if k == 0:
                cells_bf, outs = outs[0], outs[1:]
            if k == CHUNKS - 1:
                grad_send, grad_keep = outs
            else:
                (grad,) = outs
            if s + 1 < STRATA:
                new_chunk = permuted(new_chunk, "cell", lambda i: i - 1)
            sent.append(new_chunk)
        chunks = sent
        grad_mine = grad_keep + permuted(grad_send, "region", lambda i: i ^ bits[0])
        grad_mine = summed(grad_mine, bits[1:], index, s)
        mom_mine = grad_mine if s == 0 else beta_mom * mom_mine + grad_mine
        mom_other = permuted(mom_mine, "region", lambda i: i ^ bits[0])
    regions = returned(chunks)
    mom = jnp.concatenate(
        [jnp.where(side == 0, mom_mine, mom_other), jnp.where(side == 0, mom_other, mom_mine)], 0
    )
    return (cells_now - mom, regions)


def solution(mesh):
    in_specs = (
        P("cell", "region"),
        P("cell", "region"),
        P(),
        P("cell", None),
        P(("cell", "region"), None),
    )
    out_specs = (P("cell", None), P(("cell", "region"), None))

    return jax.shard_map(body, mesh=mesh, in_specs=in_specs, out_specs=out_specs, check_vma=False)
```
